128 devices in a mesh: sector: 32 (over z, y, x_hi), axial: 2 (over core), radial: 2 (over x_lo).
Axes of the slice: x: 4 (x_hi: 2, x_lo: 2; x = x_hi * 2 + x_lo), y: 4, z: 4, core: 2. Of those that a mesh axis runs over, the one named last changes fastest.
Arguments:
- state: float32 [64, 5, 16, 4096], P('axial', None, 'radial', 'sector'), may hold values from -6 to 6
- block_inverse: float32 [64, 5, 5, 16, 4096], P('axial', None, None, 'radial', 'sector'), may hold values from -2.1 to 2.1
- lower_rate: float32 [64, 16, 4096], P('axial', 'radial', 'sector'), may hold values from 0.5 to 2
- upper_rate: float32 [64, 16, 4096], P('axial', 'radial', 'sector'), may hold values from 0.5 to 2
- lower_jac: float32 [5, 5], replicated, may hold values from -1 to 1, as said below
- upper_jac: float32 [5, 5], replicated, may hold values from -1 to 1, as said below
- parcel_state: float32 [6, 2, 2, 1048576], P(None, 'axial', 'radial', 'sector'), may hold values from -4 to 4, as said below
- parcel_cell: int32 [2, 2, 1048576], P('axial', 'radial', 'sector'), may hold values from 0 to 32639
- parcel_count: int32 [2, 2, 32], P('axial', 'radial', 'sector'), may hold values from 4096 to 32768, as said below
Outputs:
- state_next: float32 [64, 5, 16, 4096], P('axial', None, 'radial', 'sector')
- parcel_left: float32 [2, 2, 1048576], P('axial', 'radial', 'sector')
The draws below stay inside these ranges and needn't reach their ends.
Inputs may be any that keep to these rules, and one draw needn't show every extreme that they name: `parcel_count`: some block has all 32768 slots live. `lower_jac`: symmetric. `upper_jac`: symmetric. `parcel_state`: fields 0 and 1 are positive.
All inputs are finite; a program needn't handle non-finite values.
Results may differ from the reference program's by a relative error of at most 0.00021.
Values sent between devices are 32-bit elements; how exact they have to be, the bound alone decides.
A program may use at most 128 MiB of HBM per device.

```python
import jax
import jax.numpy as jnp
from jax import lax

NV = 5
NPF = 6
SWEEPS = 2
CX = 32
CR = 8
CA = 128
PSLOT = 32768
NX = 64
NR = 16
NA = 4096
NXB = 2
NRB = 2
NSEC = 32
SLOTS = 1048576


def face_rates(key):
    base = jax.random.fold_in(key, 11)
    spread = jax.random.uniform(base, (2, NX, NR, NA), jnp.float32)
    return jnp.exp(jnp.log(0.5) + jnp.log(4.0) * spread)


def mode_basis(key):
    base = jax.random.fold_in(key, 23)
    first, second, third = jax.random.split(base, 3)
    magnitude = 0.5 + jax.random.uniform(first, (NV,), jnp.float32)
    flips = jax.random.uniform(second, (NV,), jnp.float32)
    vector = jnp.where(flips < 0.5, -magnitude, magnitude)
    unit = vector / jnp.sqrt(jnp.sum(vector * vector))
    middle = jax.random.uniform(third, (NV - 2,), jnp.float32, -0.9, 0.9)
    edge = 1.0 - 0.5 / CX
    speeds = jnp.concatenate([jnp.array([edge, -edge], jnp.float32), middle])
    return (unit, 0.5 * (1.0 + speeds), 0.5 * (1.0 - speeds))


def reflected(unit, values):
    extra = (1,) * (values.ndim - 1)
    column = unit.reshape((NV,) + extra)
    left_u = column[:, None]
    right_u = column[None, :]
    weight = jnp.sum(values * column * column, axis=0)
    identity = jnp.eye(NV, dtype=jnp.float32).reshape((NV, NV) + extra)
    left_v = values[:, None]
    right_v = values[None, :]
    return identity * left_v - 2.0 * left_u * right_u * (left_v + right_v) + 4.0 * weight[None, None] * left_u * right_u


def draw_lower_rate(key, part):
    return face_rates(key)[0]


def draw_upper_rate(key, part):
    return face_rates(key)[1]


def draw_lower_jac(key, part):
    unit, lower, upper = mode_basis(key)
    return reflected(unit, lower)


def draw_upper_jac(key, part):
    unit, lower, upper = mode_basis(key)
    return reflected(unit, upper)


def draw_block_inverse(key, part):
    rates = face_rates(key)
    unit, lower, upper = mode_basis(key)
    damping = 0.25 / CX
    diagonal = damping + lower.reshape(NV, 1, 1, 1) * rates[0][None] + upper.reshape(NV, 1, 1, 1) * rates[1][None]
    inverse = reflected(unit, 1.0 / diagonal)
    noise = jax.random.uniform(jax.random.fold_in(key, 37), (NX, NV, NV, NR, NA), jnp.float32, -0.05, 0.05)
    return jnp.transpose(inverse, (2, 0, 1, 3, 4)) + noise


def draw_parcel_state(key, part):
    first, second = jax.random.split(key, 2)
    spread = jax.random.uniform(first, (2, NXB, NRB, SLOTS), jnp.float32)
    mass = jnp.exp(jnp.log(0.05) * (1.0 - spread[0]))
    rate = jnp.exp(jnp.log(0.1) + jnp.log(20.0) * spread[1])
    motion = jax.random.truncated_normal(second, -4.0, 4.0, (4, NXB, NRB, SLOTS), jnp.float32)
    return jnp.concatenate([mass[None], rate[None], motion], axis=0)


def draw_parcel_count(key, part):
    keys = jax.random.split(key, 4)
    shape = (NXB, NRB, NSEC)
    sparse = jax.random.randint(keys[0], shape, PSLOT // 8, PSLOT // 2 + 1)
    dense = jax.random.randint(keys[1], shape, PSLOT // 2, PSLOT + 1)
    near = jax.random.randint(keys[2], (1, 1, NSEC), 0, 2)
    counts = jnp.where(near == 1, dense, sparse)
    chosen = jax.random.randint(keys[3], (), 0, NSEC)
    first_x = lax.broadcasted_iota(jnp.int32, shape, 0) == 0
    first_r = lax.broadcasted_iota(jnp.int32, shape, 1) == 0
    picked = lax.broadcasted_iota(jnp.int32, shape, 2) == chosen
    return jnp.where(first_x & first_r & picked, PSLOT, counts).astype(jnp.int32)


def set_ends(values, rng, least, top_value):
    longest = values.shape.index(max(values.shape))
    spots = []
    for shift in (0, 1):
        where = [jax.random.randint(jax.random.fold_in(rng, axis), (), 0, length) for axis, length in enumerate(values.shape)]
        where[longest] = (where[longest] + shift) % values.shape[longest]
        spots.append(tuple(where))
    return values.at[spots[0]].set(least).at[spots[1]].set(top_value)


def shard_levels(key, dims, shards, smallest, largest):
    def one(dim, shards_of):
        steps = jax.random.uniform(jax.random.fold_in(jax.random.fold_in(key, 6), dim), (shards_of,), jnp.float32, smallest / len(shards), largest / len(shards))
        return jnp.repeat(jnp.exp(steps), dims[dim] // shards_of).reshape((-1,) + (1,) * (len(dims) - dim - 1))

    loudness = one(*shards[0])
    for cut in shards[1:]:
        loudness = loudness * one(*cut)
    return loudness


def bell_draw(own_key, extent, scale, most, pieces=(), kind=jnp.bfloat16):
    values = jax.random.normal(own_key, extent, jnp.float32) * scale
    if len(pieces) > 0:
        values = shard_levels(own_key, extent, pieces, -0.22, 0.18) * values
    return jnp.clip(values, min=-most, max=most).astype(kind)


def setup_inputs(seed: int = 0) -> dict:
    streams_of = jax.random.split(jax.random.key(seed), 10)
    state = bell_draw(streams_of[0], (NX, NV, NR, NA), 1.0, 6.0, ((0, 2), (2, 2), (3, 32)), jnp.float32)
    block_inverse = draw_block_inverse(jax.random.fold_in(streams_of[9], 71), 0)
    lower_rate = draw_lower_rate(jax.random.fold_in(streams_of[9], 71), 0)
    upper_rate = draw_upper_rate(jax.random.fold_in(streams_of[9], 71), 0)
    lower_jac = draw_lower_jac(jax.random.fold_in(streams_of[9], 71), 0)
    upper_jac = draw_upper_jac(jax.random.fold_in(streams_of[9], 71), 0)
    parcel_state = draw_parcel_state(jax.random.fold_in(streams_of[9], 71), 0)
    parcel_cell = set_ends(jax.random.randint(streams_of[7], (NXB, NRB, SLOTS), 0, min(CX * CR * CA - CA, 65280)), jax.random.fold_in(streams_of[7], 1), 0, (min(CX * CR * CA - CA, 65280)) - 1).astype(jnp.int32)
    parcel_count = draw_parcel_count(jax.random.fold_in(streams_of[9], 71), 0)
    return dict(state=state, block_inverse=block_inverse, lower_rate=lower_rate, upper_rate=upper_rate, lower_jac=lower_jac, upper_jac=upper_jac, parcel_state=parcel_state, parcel_cell=parcel_cell, parcel_count=parcel_count)


HIGH = lax.Precision.HIGHEST
DIFFUSE = 0.15
SWIRL = 0.6


def sweep(inflow, inverse, targets, rates, jac, reverse):
    def step(carry, inputs):
        block, target, rate = inputs
        pushed = jnp.einsum('uv,vrc->urc', jac, carry, precision=HIGH)
        value = jnp.einsum('uvrc,vrc->urc', block, target - rate[None] * pushed, precision=HIGH)
        return value, value
    return lax.scan(step, inflow, (inverse, targets, rates), reverse=reverse)


def reference(state, block_inverse, lower_rate, upper_rate, lower_jac, upper_jac, parcel_state, parcel_cell, parcel_count):
    padded = jnp.pad(state, ((1, 1), (0, 0), (1, 1), (0, 0)))
    below = jnp.roll(state, 1, axis=3)
    above = jnp.roll(state, -1, axis=3)
    beside = padded[2:, :, 1:-1] + padded[:-2, :, 1:-1] + padded[1:-1, :, 2:] + padded[1:-1, :, :-2] + below + above
    flux = DIFFUSE * (beside - 6.0 * state) + SWIRL * (below - state)

    arrived = jnp.roll(parcel_state.reshape(NPF, NXB, NRB, NSEC, PSLOT), 1, axis=3)
    cells = parcel_cell.reshape(NXB, NRB, NSEC, PSLOT)
    plane = cells // (CR * CA)
    local_r = (cells // CA) % CR
    local_a = cells % CA
    glob_x = jnp.arange(NXB, dtype=jnp.int32)[:, None, None, None] * CX + plane
    glob_r = jnp.arange(NRB, dtype=jnp.int32)[None, :, None, None] * CR + local_r
    glob_a = jnp.arange(NSEC, dtype=jnp.int32)[None, None, :, None] * CA + local_a
    flat = ((glob_x * NR + glob_r) * NA + glob_a).reshape(-1).astype(jnp.int32)
    slot = jnp.arange(PSLOT, dtype=jnp.int32)[None, None, None, :]
    live = (slot < parcel_count[..., None]).astype(jnp.float32).reshape(-1)
    fields = arrived.reshape(NPF, -1)
    gas = state[:, 4].reshape(-1)[flat]
    frac = 1.0 - jnp.exp(-fields[1] * (1.0 + 0.5 * jnp.tanh(gas)))
    evap = live * fields[0] * frac
    parcel_left = (live * fields[0] * (1.0 - frac)).reshape(NXB, NRB, SLOTS)
    deposits = jnp.stack([evap, evap * fields[2], evap * fields[3], evap * fields[4], evap * fields[5]], axis=1)
    source = jax.ops.segment_sum(deposits, flat, num_segments=NX * NR * NA)
    source = source.reshape(NX, NR, NA, NV).transpose(0, 3, 1, 2)
    residual = flux + source

    update = jnp.zeros_like(state)
    face = jnp.zeros((NV, NR, NA), jnp.float32)
    for sweep_index in range(SWEEPS):
        ahead = jnp.concatenate([update[1:], face[None]], axis=0)
        targets = residual - upper_rate[:, None] * jnp.einsum('uv,kvrc->kurc', upper_jac, ahead, precision=HIGH)
        last, starred = sweep(face, block_inverse, targets, lower_rate, lower_jac, False)
        behind = jnp.concatenate([face[None], starred[:-1]], axis=0)
        targets = residual - lower_rate[:, None] * jnp.einsum('uv,kvrc->kurc', lower_jac, behind, precision=HIGH)
        first, update = sweep(face, block_inverse, targets, upper_rate, upper_jac, True)
    return state + update, parcel_left
```

```python
import functools

import jax
import jax.numpy as jnp
from jax import lax
from jax.experimental import pallas as pl
from jax.experimental.pallas import tpu as pltpu
from jax.sharding import PartitionSpec as P

F32 = jnp.float32
BF = jnp.bfloat16
MESH = pl.DeviceIdType.MESH
NT = (((1,), (1,)), ((), ()))
DIFFUSE = 0.15
SWIRL = 0.6
CH = 16


def sum5(terms):
    return ((terms[0] + terms[1]) + (terms[2] + terms[3])) + terms[4]


def rows16(row, times):
    packed = jnp.broadcast_to(row, (16, 128)).astype(BF)
    return jnp.concatenate([packed] * times, axis=0)


def one_hots(cells, oh, mk):
    row = lax.shift_right_logical(cells, 7).astype(F32)
    lane = (cells & 127).astype(F32)
    index = lax.broadcasted_iota(jnp.int32, (256, 128), 0).astype(F32).astype(BF)
    one, zero = jnp.ones((), BF), jnp.zeros((), BF)
    for j in range(CH):
        at = slice(j * 128, (j + 1) * 128)
        oh[:, at] = jnp.where(index == rows16(row[j : j + 1], 16), one, zero)
        mk[:, at] = jnp.where(index[:128] == rows16(lane[j : j + 1], 8), one, zero)


def kernel(
    nsec,
    state, binv, lrate, urate, ljac, ujac, parcels, cell, count,
    out, left,
    sx, bv, lv, uv, cv, pbuf, gas, g2, oh, mk, w, acc, res, tgt, edge,
    rsend, rrecv, upsend, uprecv, dnsend, dnrecv, face, fsend,
    lsem, psend, precv, hsend, hrecv, rlsend, rlrecv,
):
    s, a, r = lax.axis_index("sector"), lax.axis_index("axial"), lax.axis_index("radial")
    nxt, prv = lax.rem(s + 1, nsec), lax.rem(s + nsec - 1, nsec)
    steps = 256 // CH

    local = [
        pltpu.make_async_copy(state, sx.at[pl.ds(5, 160)], lsem.at[0]),
        pltpu.make_async_copy(cell, cv, lsem.at[1]),
        pltpu.make_async_copy(binv, bv, lsem.at[2]),
        pltpu.make_async_copy(lrate, lv, lsem.at[3]),
        pltpu.make_async_copy(urate, uv, lsem.at[4]),
    ]
    for copy in local:
        copy.start()

    barrier = pltpu.get_barrier_semaphore()
    for device in ((nxt, a, r), (prv, a, r), (s, 1 - a, r), (s, a, 1 - r)):
        pl.semaphore_signal(barrier, inc=1, device_id=device, device_id_type=MESH)
    pl.semaphore_wait(barrier, 4)

    def remote(src, dst, ssem, rsem, device):
        return pltpu.make_async_remote_copy(
            src_ref=src, dst_ref=dst, send_sem=ssem, recv_sem=rsem, device_id=device, device_id_type=MESH
        )

    def parcel_copy(c):
        rows = pl.ds(pl.multiple_of(c * CH, CH), CH)
        return remote(parcels.at[:, rows], pbuf.at[:, rows], psend.at[c], precv.at[c], (nxt, a, r))

    local[0].wait()

    def pack_radial(k, carry):
        rows = [
            jnp.where(r == 0, sx[5 + k * 5 + u, 7:8, :], sx[5 + k * 5 + u, 0:1, :]) for u in range(5)
        ]
        rsend[k] = jnp.concatenate(rows + [jnp.zeros((3, 128), F32)], axis=0)
        return carry

    lax.fori_loop(0, 32, pack_radial, 0)
    for q in range(10):
        turned = sx[5 + 16 * q : 21 + 16 * q].reshape(128, 128).T
        upsend[q : q + 1] = turned[127:128]
        dnsend[q : q + 1] = turned[0:1]
    halo = [
        remote(state.at[pl.ds(155 * (1 - a), 5)], sx.at[pl.ds(165 * a, 5)], hsend.at[0], hrecv.at[0], (s, 1 - a, r)),
        remote(rsend, rrecv, hsend.at[1], hrecv.at[1], (s, a, 1 - r)),
        remote(upsend, uprecv, hsend.at[2], hrecv.at[2], (nxt, a, r)),
        remote(dnsend, dnrecv, hsend.at[3], hrecv.at[3], (prv, a, r)),
    ]
    for copy in halo:
        copy.start()

    def send_parcels(c, carry):
        parcel_copy(c).start()
        return carry

    lax.fori_loop(0, steps, send_parcels, 0)

    for h in range(2):
        tile = jnp.concatenate([sx[5 + (16 * h + k) * 5 + 4] for k in range(16)], axis=0)
        turned = tile.T
        hi = turned.astype(BF)
        g2[0:128, h * 128 : (h + 1) * 128] = hi
        g2[128:256, h * 128 : (h + 1) * 128] = (turned - hi.astype(F32)).astype(BF)
    local[1].wait()

    def gather(i, carry):
        rows = pl.ds(pl.multiple_of(i * CH, CH), CH)
        one_hots(cv[rows], oh, mk)
        found = jnp.dot(g2[...], oh[...], preferred_element_type=F32)
        picked = (found[:128] + found[128:]) * mk[...].astype(F32)
        total = jnp.sum(jnp.sum(picked.reshape(16, 8, CH * 128), axis=0), axis=0, keepdims=True)
        for j in range(CH):
            gas[pl.ds(i * CH + j, 1), :] = total[:, j * 128 : (j + 1) * 128]
        return carry

    lax.fori_loop(0, steps, gather, 0)

    @pl.when(a == 0)
    def _():
        sx[0:5] = jnp.zeros((5, 8, 128), F32)

    @pl.when(a == 1)
    def _():
        sx[165:170] = jnp.zeros((5, 8, 128), F32)

    for copy in halo:
        copy.wait_recv()
    sub = lax.broadcasted_iota(jnp.int32, (128, 128), 0)
    for q in range(10):
        both = jnp.where(
            sub == 0,
            (DIFFUSE + SWIRL) * uprecv[q : q + 1],
            jnp.where(sub == 127, DIFFUSE * dnrecv[q : q + 1], 0.0),
        )
        edge[16 * q : 16 * q + 16] = both.T.reshape(16, 8, 128)
    sub8 = lax.broadcasted_iota(jnp.int32, (8, 128), 0)
    lane8 = lax.broadcasted_iota(jnp.int32, (8, 128), 1)
    seam = sub8 == 7 * (1 - r)

    def flux(k, carry):
        ring = rrecv[k]
        for u in range(5):
            i = k * 5 + u
            x = sx[5 + i]
            radial = (
                jnp.where(sub8 == 0, 0.0, pltpu.roll(x, 1, 0))
                + jnp.where(sub8 == 7, 0.0, pltpu.roll(x, 7, 0))
                + jnp.where(seam, jnp.broadcast_to(ring[u : u + 1], (8, 128)), 0.0)
            )
            below = jnp.where(lane8 == 0, 0.0, pltpu.roll(x, 1, 1))
            above = jnp.where(lane8 == 127, 0.0, pltpu.roll(x, 127, 1))
            beside = (sx[i] + sx[i + 10]) + (radial + above)
            res[i] = (
                DIFFUSE * beside + (DIFFUSE + SWIRL) * below + edge[i] - (6.0 * DIFFUSE + SWIRL) * x
            )
        return carry

    lax.fori_loop(0, 32, flux, 0)

    acc[...] = jnp.zeros_like(acc)
    live_count = count[0]

    def scatter(i, carry):
        parcel_copy(i).wait_recv()
        rows = pl.ds(pl.multiple_of(i * CH, CH), CH)
        one_hots(cv[rows], oh, mk)
        fields = [pbuf[f, rows] for f in range(6)]
        slot = (lax.broadcasted_iota(jnp.int32, (CH, 128), 0) + i * CH) * 128 + lax.broadcasted_iota(
            jnp.int32, (CH, 128), 1
        )
        mass = jnp.where(slot < live_count, fields[0], 0.0)
        frac = 1.0 - jnp.exp(-fields[1] * (1.0 + 0.5 * jnp.tanh(gas[rows])))
        evap = mass * frac
        left[rows] = mass * (1.0 - frac)
        deposits = [evap] + [evap * fields[f] for f in range(2, 6)]
        for v in range(5):
            hi = deposits[v].astype(BF).astype(F32)
            for half, piece in enumerate((hi, deposits[v] - hi)):
                for j in range(CH):
                    at = (half * CH + j) * 128
                    w[v * 128 : (v + 1) * 128, at : at + 128] = mk[:, j * 128 : (j + 1) * 128] * rows16(
                        piece[j : j + 1], 8
                    )
        width = CH * 128
        acc[...] += lax.dot_general(w[:, :width], oh[...], NT, preferred_element_type=F32) + lax.dot_general(
            w[:, width:], oh[...], NT, preferred_element_type=F32
        )
        return carry

    lax.fori_loop(0, steps, scatter, 0)
    for v in range(5):
        turned = acc[v * 128 : (v + 1) * 128].T
        for k in range(32):
            res[k * 5 + v] += turned[8 * k : 8 * k + 8]

    for copy in local[2:]:
        copy.wait()
    zeros = tuple(jnp.zeros((8, 128), F32) for _ in range(5))

    def product(jac, values):
        return [sum5([jac[u, v] * values[v] for v in range(5)]) for u in range(5)]

    def plane(k, carry, rate, jac, first, final):
        pushed = product(jac, carry)
        base = k * 5
        rk = rate[k]
        net = []
        for u in range(5):
            term = rk * pushed[u]
            r_u = res[base + u]
            if first:
                d = r_u - term
                tgt[base + u] = d
            else:
                d = tgt[base + u] - term
                if not final:
                    tgt[base + u] = r_u - term
            net.append(d)
        value = tuple(sum5([bv[k * 25 + u * 5 + v] * net[v] for v in range(5)]) for u in range(5))
        if final:
            for u in range(5):
                out[base + u] = sx[5 + base + u] + value[u]
        return value

    def relay(h):
        return remote(fsend.at[h], face.at[h], rlsend.at[h], rlrecv.at[h], (s, 1 - a, r))

    def half_sweep(hop, forward, first, final):
        sender = 0 if forward else 1

        @pl.when(a == 1 - sender)
        def _():
            relay(hop).wait_recv()

        @pl.when(a == sender)
        def _():
            face[hop] = jnp.zeros((5, 8, 128), F32)

        inflow = tuple(face[hop, u] for u in range(5))
        rate, jac = (lv, ljac) if forward else (uv, ujac)

        def body(i, carry):
            k = i if forward else 31 - i
            return plane(k, carry, rate, jac, first, final)

        last = lax.fori_loop(0, 32, body, inflow)

        @pl.when(a == sender)
        def _():
            for u in range(5):
                fsend[hop, u] = last[u]
            relay(hop).start()

    half_sweep(0, True, True, False)
    half_sweep(1, False, False, False)
    half_sweep(2, True, False, False)
    half_sweep(3, False, False, True)

    for hop in range(4):
        @pl.when(a == hop % 2)
        def _():
            relay(hop).wait_send()

    for copy in halo:
        copy.wait_send()

    def sent(c, carry):
        parcel_copy(c).wait_send()
        return carry

    lax.fori_loop(0, steps, sent, 0)


def solution(mesh):
    nsec = mesh.shape["sector"]

    def local(state, block_inverse, lower_rate, upper_rate, lower_jac, upper_jac, parcel_state, parcel_cell, parcel_count):
        hbm = pl.BlockSpec(memory_space=pl.ANY)
        vmem = pl.BlockSpec(memory_space=pltpu.VMEM)
        smem = pl.BlockSpec(memory_space=pltpu.SMEM)
        width = CH * 128
        dma = pltpu.SemaphoreType.DMA
        steps = 256 // CH
        out, left = pl.pallas_call(
            functools.partial(kernel, nsec),
            out_shape=(
                jax.ShapeDtypeStruct((160, 8, 128), F32),
                jax.ShapeDtypeStruct((256, 128), F32),
            ),
            in_specs=[hbm, hbm, hbm, hbm, smem, smem, hbm, hbm, smem],
            out_specs=(vmem, vmem),
            scratch_shapes=[
                pltpu.VMEM((170, 8, 128), F32),
                pltpu.VMEM((800, 8, 128), F32),
                pltpu.VMEM((32, 8, 128), F32),
                pltpu.VMEM((32, 8, 128), F32),
                pltpu.VMEM((256, 128), jnp.int32),
                pltpu.VMEM((6, 256, 128), F32),
                pltpu.VMEM((256, 128), F32),
                pltpu.VMEM((256, 256), BF),
                pltpu.VMEM((256, width), BF),
                pltpu.VMEM((128, width), BF),
                pltpu.VMEM((640, 2 * width), BF),
                pltpu.VMEM((640, 256), F32),
                pltpu.VMEM((160, 8, 128), F32),
                pltpu.VMEM((160, 8, 128), F32),
                pltpu.VMEM((160, 8, 128), F32),
                pltpu.VMEM((32, 8, 128), F32),
                pltpu.VMEM((32, 8, 128), F32),
                pltpu.VMEM((16, 128), F32),
                pltpu.VMEM((16, 128), F32),
                pltpu.VMEM((16, 128), F32),
                pltpu.VMEM((16, 128), F32),
                pltpu.VMEM((4, 5, 8, 128), F32),
                pltpu.VMEM((4, 5, 8, 128), F32),
                dma((5,)),
                dma((steps,)),
                dma((steps,)),
                dma((4,)),
                dma((4,)),
                dma((4,)),
                dma((4,)),
            ],
            compiler_params=pltpu.CompilerParams(
                collective_id=0, has_side_effects=True, vmem_limit_bytes=56 << 20
            ),
        )(
            state.reshape(160, 8, 128),
            block_inverse.reshape(800, 8, 128),
            lower_rate,
            upper_rate,
            lower_jac,
            upper_jac,
            parcel_state.reshape(6, 256, 128),
            parcel_cell.reshape(256, 128),
            parcel_count.reshape(1),
        )
        return out.reshape(state.shape), left.reshape(parcel_cell.shape)

    return jax.shard_map(
        local,
        mesh=mesh,
        in_specs=(
            P("axial", None, "radial", "sector"),
            P("axial", None, None, "radial", "sector"),
            P("axial", "radial", "sector"),
            P("axial", "radial", "sector"),
            P(),
            P(),
            P(None, "axial", "radial", "sector"),
            P("axial", "radial", "sector"),
            P("axial", "radial", "sector"),
        ),
        out_specs=(P("axial", None, "radial", "sector"), P("axial", "radial", "sector")),
        check_vma=False,
    )
```

```python
import functools

import jax
import jax.numpy as jnp
from jax import lax
from jax.experimental import pallas as pl
from jax.experimental.pallas import tpu as pltpu
from jax.sharding import PartitionSpec as P

F32 = jnp.float32
BF = jnp.bfloat16
F8 = jnp.float8_e4m3fn
MESH = pl.DeviceIdType.MESH
NT = (((1,), (1,)), ((), ()))
DIFFUSE = 0.15
SWIRL = 0.6
CH = 32
LOW = 8192.0


def sum5(terms):
    return ((terms[0] + terms[1]) + (terms[2] + terms[3])) + terms[4]


def rows16(row, times):
    packed = jnp.broadcast_to(row, (16, 128)).astype(BF)
    return jnp.concatenate([packed] * times, axis=0)


def one_hots(cells, i, oh, oh8, mk):
    row = lax.shift_right_logical(cells, 7).astype(F32)
    lane = (cells & 127).astype(F32)
    index = lax.broadcasted_iota(jnp.int32, (256, 128), 0).astype(F32).astype(BF)
    one, zero = jnp.ones((), BF), jnp.zeros((), BF)
    for j in range(CH):
        at = slice(j * 128, (j + 1) * 128)
        hot = jnp.where(index == rows16(row[j : j + 1], 16), one, zero)
        oh[i, :, at] = hot
        oh8[i, :, at] = hot.astype(F8)
        mk[i, :, at] = jnp.where(index[:128] == rows16(lane[j : j + 1], 8), one, zero)


def kernel(
    nsec,
    state, binv, lrate, urate, ljac, ujac, parcels, cell, count,
    out, left,
    sx, bv, lv, uv, cv, pbuf, gas, g2, oh, oh8, mk, w, w8, acc, res, tgt, edge,
    rsend, rrecv, upsend, uprecv, dnsend, dnrecv, face, fsend,
    lsem, psend, precv, hsend, hrecv, rlsend, rlrecv,
):
    s, a, r = lax.axis_index("sector"), lax.axis_index("axial"), lax.axis_index("radial")
    nxt, prv = lax.rem(s + 1, nsec), lax.rem(s + nsec - 1, nsec)
    steps = 256 // CH

    local = [
        pltpu.make_async_copy(state, sx.at[pl.ds(5, 160)], lsem.at[0]),
        pltpu.make_async_copy(cell, cv, lsem.at[1]),
        pltpu.make_async_copy(binv, bv, lsem.at[2]),
        pltpu.make_async_copy(lrate, lv, lsem.at[3]),
        pltpu.make_async_copy(urate, uv, lsem.at[4]),
    ]
    for copy in local:
        copy.start()

    barrier = pltpu.get_barrier_semaphore()
    for device in ((nxt, a, r), (prv, a, r), (s, 1 - a, r), (s, a, 1 - r)):
        pl.semaphore_signal(barrier, inc=1, device_id=device, device_id_type=MESH)

    def remote(src, dst, ssem, rsem, device):
        return pltpu.make_async_remote_copy(
            src_ref=src, dst_ref=dst, send_sem=ssem, recv_sem=rsem, device_id=device, device_id_type=MESH
        )

    def parcel_copy(c):
        rows = pl.ds(pl.multiple_of(c * CH, CH), CH)
        return remote(parcels.at[:, rows], pbuf.at[:, rows], psend.at[c], precv.at[c], (nxt, a, r))

    local[0].wait()

    for i in range(160):
        rsend[i : i + 1] = jnp.where(r == 0, sx[5 + i, 7:8, :], sx[5 + i, 0:1, :])
    for q in range(10):
        turned = sx[5 + 16 * q : 21 + 16 * q].reshape(128, 128).T
        upsend[q : q + 1] = turned[127:128]
        dnsend[q : q + 1] = turned[0:1]
    for h in range(2):
        tile = jnp.concatenate([sx[5 + (16 * h + k) * 5 + 4] for k in range(16)], axis=0)
        turned = tile.T
        hi = turned.astype(BF)
        g2[0:128, h * 128 : (h + 1) * 128] = hi
        g2[128:256, h * 128 : (h + 1) * 128] = (turned - hi.astype(F32)).astype(BF)
    pl.semaphore_wait(barrier, 4)
    halo = [
        remote(state.at[pl.ds(155 * (1 - a), 5)], sx.at[pl.ds(165 * a, 5)], hsend.at[0], hrecv.at[0], (s, 1 - a, r)),
        remote(rsend, rrecv, hsend.at[1], hrecv.at[1], (s, a, 1 - r)),
        remote(upsend, uprecv, hsend.at[2], hrecv.at[2], (nxt, a, r)),
        remote(dnsend, dnrecv, hsend.at[3], hrecv.at[3], (prv, a, r)),
    ]
    for copy in halo:
        copy.start()

    def send_parcels(c, carry):
        parcel_copy(c).start()
        return carry

    lax.fori_loop(0, steps, send_parcels, 0)

    local[1].wait()

    def gather(i, carry):
        rows = pl.ds(pl.multiple_of(i * CH, CH), CH)
        one_hots(cv[rows], i, oh, oh8, mk)
        found = jnp.dot(g2[...], oh[i], preferred_element_type=F32)
        picked = (found[:128] + found[128:]) * mk[i].astype(F32)
        total = jnp.sum(jnp.sum(picked.reshape(16, 8, CH * 128), axis=0), axis=0, keepdims=True)
        for j in range(CH):
            gas[pl.ds(i * CH + j, 1), :] = total[:, j * 128 : (j + 1) * 128]
        return carry

    lax.fori_loop(0, steps, gather, 0)

    @pl.when(a == 0)
    def _():
        sx[0:5] = jnp.zeros((5, 8, 128), F32)

    @pl.when(a == 1)
    def _():
        sx[165:170] = jnp.zeros((5, 8, 128), F32)

    for copy in halo:
        copy.wait_recv()
    sub = lax.broadcasted_iota(jnp.int32, (128, 128), 0)
    for q in range(10):
        both = jnp.where(
            sub == 0,
            (DIFFUSE + SWIRL) * uprecv[q : q + 1],
            jnp.where(sub == 127, DIFFUSE * dnrecv[q : q + 1], 0.0),
        )
        edge[16 * q : 16 * q + 16] = both.T.reshape(16, 8, 128)
    sub8 = lax.broadcasted_iota(jnp.int32, (8, 128), 0)
    lane8 = lax.broadcasted_iota(jnp.int32, (8, 128), 1)
    seam = sub8 == 7 * (1 - r)

    def flux(k, carry):
        for u in range(5):
            i = k * 5 + u
            x = sx[5 + i]
            radial = (
                jnp.where(sub8 == 0, 0.0, pltpu.roll(x, 1, 0))
                + jnp.where(sub8 == 7, 0.0, pltpu.roll(x, 7, 0))
                + jnp.where(seam, jnp.broadcast_to(rrecv[pl.ds(i, 1)], (8, 128)), 0.0)
            )
            below = jnp.where(lane8 == 0, 0.0, pltpu.roll(x, 1, 1))
            above = jnp.where(lane8 == 127, 0.0, pltpu.roll(x, 127, 1))
            beside = (sx[i] + sx[i + 10]) + (radial + above)
            res[i] = (
                DIFFUSE * beside + (DIFFUSE + SWIRL) * below + edge[i] - (6.0 * DIFFUSE + SWIRL) * x
            )
        return carry

    lax.fori_loop(0, 32, flux, 0, unroll=4)

    acc[...] = jnp.zeros_like(acc)
    live_count = count[0]

    def scatter(i, carry):
        parcel_copy(i).wait_recv()
        rows = pl.ds(pl.multiple_of(i * CH, CH), CH)
        fields = [pbuf[f, rows] for f in range(6)]
        slot = (lax.broadcasted_iota(jnp.int32, (CH, 128), 0) + i * CH) * 128 + lax.broadcasted_iota(
            jnp.int32, (CH, 128), 1
        )
        mass = jnp.where(slot < live_count, fields[0], 0.0)
        frac = 1.0 - jnp.exp(-fields[1] * (1.0 + 0.5 * jnp.tanh(gas[rows])))
        evap = mass * frac
        left[rows] = mass * (1.0 - frac)
        deposits = [evap] + [evap * fields[f] for f in range(2, 6)]
        for v in range(5):
            hi = deposits[v].astype(BF).astype(F32)
            low = (deposits[v] - hi) * LOW
            for j in range(CH):
                at = slice(j * 128, (j + 1) * 128)
                hot = mk[i, :, at]
                w[v * 128 : (v + 1) * 128, at] = hot * rows16(hi[j : j + 1], 8)
                w8[v * 128 : (v + 1) * 128, at] = (hot * rows16(low[j : j + 1], 8)).astype(F8)
        acc[:640] += lax.dot_general(w[...], oh[i], NT, preferred_element_type=F32)
        acc[640:] += lax.dot_general(w8[...], oh8[i], NT, preferred_element_type=F32)
        return carry

    lax.fori_loop(0, steps, scatter, 0)
    for v in range(5):
        turned = (acc[v * 128 : (v + 1) * 128] + acc[640 + v * 128 : 768 + v * 128] * (1.0 / LOW)).T
        for k in range(32):
            res[k * 5 + v] += turned[8 * k : 8 * k + 8]

    for copy in local[2:]:
        copy.wait()
    zeros = tuple(jnp.zeros((8, 128), F32) for _ in range(5))

    def product(jac, values):
        return [sum5([jac[u, v] * values[v] for v in range(5)]) for u in range(5)]

    def plane(k, carry, rate, jac, first, final):
        pushed = product(jac, carry)
        base = k * 5
        rk = rate[k]
        net = []
        for u in range(5):
            term = rk * pushed[u]
            r_u = res[base + u]
            if first:
                d = r_u - term
                tgt[base + u] = d
            else:
                d = tgt[base + u] - term
                if not final:
                    tgt[base + u] = r_u - term
            net.append(d)
        value = tuple(sum5([bv[k * 25 + u * 5 + v] * net[v] for v in range(5)]) for u in range(5))
        if final:
            for u in range(5):
                out[base + u] = sx[5 + base + u] + value[u]
        return value

    def relay(h):
        return remote(fsend.at[h], face.at[h], rlsend.at[h], rlrecv.at[h], (s, 1 - a, r))

    def half_sweep(hop, forward, first, final):
        sender = 0 if forward else 1

        @pl.when(a == 1 - sender)
        def _():
            relay(hop).wait_recv()

        @pl.when(a == sender)
        def _():
            face[hop] = jnp.zeros((5, 8, 128), F32)

        inflow = tuple(face[hop, u] for u in range(5))
        rate, jac = (lv, ljac) if forward else (uv, ujac)

        def body(i, carry):
            k = i if forward else 31 - i
            return plane(k, carry, rate, jac, first, final)

        last = lax.fori_loop(0, 32, body, inflow, unroll=4)

        @pl.when(a == sender)
        def _():
            for u in range(5):
                fsend[hop, u] = last[u]
            relay(hop).start()

    half_sweep(0, True, True, False)
    half_sweep(1, False, False, False)
    half_sweep(2, True, False, False)
    half_sweep(3, False, False, True)

    for hop in range(4):
        @pl.when(a == hop % 2)
        def _():
            relay(hop).wait_send()

    for copy in halo:
        copy.wait_send()

    def sent(c, carry):
        parcel_copy(c).wait_send()
        return carry

    lax.fori_loop(0, steps, sent, 0)


def solution(mesh):
    nsec = mesh.shape["sector"]

    def local(state, block_inverse, lower_rate, upper_rate, lower_jac, upper_jac, parcel_state, parcel_cell, parcel_count):
        hbm = pl.BlockSpec(memory_space=pl.ANY)
        vmem = pl.BlockSpec(memory_space=pltpu.VMEM)
        smem = pl.BlockSpec(memory_space=pltpu.SMEM)
        width = CH * 128
        dma = pltpu.SemaphoreType.DMA
        steps = 256 // CH
        out, left = pl.pallas_call(
            functools.partial(kernel, nsec),
            out_shape=(
                pltpu.VMEM((160, 8, 128), F32),
                pltpu.VMEM((256, 128), F32),
            ),
            in_specs=[hbm, hbm, hbm, hbm, smem, smem, hbm, hbm, smem],
            out_specs=(vmem, vmem),
            scratch_shapes=[
                pltpu.VMEM((170, 8, 128), F32),
                pltpu.VMEM((800, 8, 128), F32),
                pltpu.VMEM((32, 8, 128), F32),
                pltpu.VMEM((32, 8, 128), F32),
                pltpu.VMEM((256, 128), jnp.int32),
                pltpu.VMEM((6, 256, 128), F32),
                pltpu.VMEM((256, 128), F32),
                pltpu.VMEM((256, 256), BF),
                pltpu.VMEM((steps, 256, width), BF),
                pltpu.VMEM((steps, 256, width), F8),
                pltpu.VMEM((steps, 128, width), BF),
                pltpu.VMEM((640, width), BF),
                pltpu.VMEM((640, width), F8),
                pltpu.VMEM((1280, 256), F32),
                pltpu.VMEM((160, 8, 128), F32),
                pltpu.VMEM((160, 8, 128), F32),
                pltpu.VMEM((160, 8, 128), F32),
                pltpu.VMEM((160, 128), F32),
                pltpu.VMEM((160, 128), F32),
                pltpu.VMEM((16, 128), F32),
                pltpu.VMEM((16, 128), F32),
                pltpu.VMEM((16, 128), F32),
                pltpu.VMEM((16, 128), F32),
                pltpu.VMEM((4, 5, 8, 128), F32),
                pltpu.VMEM((4, 5, 8, 128), F32),
                dma((5,)),
                dma((steps,)),
                dma((steps,)),
                dma((4,)),
                dma((4,)),
                dma((4,)),
                dma((4,)),
            ],
            compiler_params=pltpu.CompilerParams(
                collective_id=0, has_side_effects=True, vmem_limit_bytes=56 << 20
            ),
        )(
            state.reshape(160, 8, 128),
            block_inverse.reshape(800, 8, 128),
            lower_rate,
            upper_rate,
            lower_jac,
            upper_jac,
            parcel_state.reshape(6, 256, 128),
            parcel_cell.reshape(256, 128),
            parcel_count.reshape(1),
        )
        return out.reshape(state.shape), left.reshape(parcel_cell.shape)

    return jax.shard_map(
        local,
        mesh=mesh,
        in_specs=(
            P("axial", None, "radial", "sector"),
            P("axial", None, None, "radial", "sector"),
            P("axial", "radial", "sector"),
            P("axial", "radial", "sector"),
            P(),
            P(),
            P(None, "axial", "radial", "sector"),
            P("axial", "radial", "sector"),
            P("axial", "radial", "sector"),
        ),
        out_specs=(P("axial", None, "radial", "sector"), P("axial", "radial", "sector")),
        check_vma=False,
    )
```

```python
import functools

import jax
import jax.numpy as jnp
from jax import lax
from jax.experimental import pallas as pl
from jax.experimental.pallas import tpu as pltpu
from jax.sharding import PartitionSpec as P

F32 = jnp.float32
BF = jnp.bfloat16
F8 = jnp.float8_e4m3fn
MESH = pl.DeviceIdType.MESH
NT = (((1,), (1,)), ((), ()))
DIFFUSE = 0.15
SWIRL = 0.6
CH = 32
EARLY = 4
LOW = 8192.0


def sum5(terms):
    return ((terms[0] + terms[1]) + (terms[2] + terms[3])) + terms[4]


def rows16(row, times):
    packed = jnp.broadcast_to(row, (16, 128)).astype(BF)
    return jnp.concatenate([packed] * times, axis=0)


def kernel(
    nsec,
    state, binv, lrate, urate, ljac, ujac, parcels, cell, count,
    out, left,
    sx, bv, lv, uv, cv, pbuf, gas, g2, oh, oh8, mk, w, w8, acc, res, tgt, edge,
    rsend, rrecv, upsend, uprecv, dnsend, dnrecv, face, fsend,
    lsem, psend, precv, hsend, hrecv, rlsend, rlrecv,
):
    s, a, r = lax.axis_index("sector"), lax.axis_index("axial"), lax.axis_index("radial")
    nxt, prv = lax.rem(s + 1, nsec), lax.rem(s + nsec - 1, nsec)
    steps = 256 // CH

    local = [
        pltpu.make_async_copy(state, sx.at[pl.ds(5, 160)], lsem.at[0]),
        pltpu.make_async_copy(cell, cv, lsem.at[1]),
        pltpu.make_async_copy(binv, bv, lsem.at[2]),
        pltpu.make_async_copy(lrate, lv, lsem.at[3]),
        pltpu.make_async_copy(urate, uv, lsem.at[4]),
    ]
    for copy in local:
        copy.start()

    barrier = pltpu.get_barrier_semaphore()
    for device in ((nxt, a, r), (prv, a, r), (s, 1 - a, r), (s, a, 1 - r)):
        pl.semaphore_signal(barrier, inc=1, device_id=device, device_id_type=MESH)

    def remote(src, dst, ssem, rsem, device):
        return pltpu.make_async_remote_copy(
            src_ref=src, dst_ref=dst, send_sem=ssem, recv_sem=rsem, device_id=device, device_id_type=MESH
        )

    def parcel_copy(c):
        rows = pl.ds(pl.multiple_of(c * CH, CH), CH)
        return remote(parcels.at[:, rows], pbuf.at[:, rows], psend.at[c], precv.at[c], (nxt, a, r))

    local[0].wait()

    for i in range(160):
        rsend[i : i + 1] = jnp.where(r == 0, sx[5 + i, 7:8, :], sx[5 + i, 0:1, :])
    for q in range(10):
        turned = sx[5 + 16 * q : 21 + 16 * q].reshape(128, 128).T
        upsend[q : q + 1] = turned[127:128]
        dnsend[q : q + 1] = turned[0:1]
    for h in range(2):
        tile = jnp.concatenate([sx[5 + (16 * h + k) * 5 + 4] for k in range(16)], axis=0)
        turned = tile.T
        hi = turned.astype(BF)
        g2[0:128, h * 128 : (h + 1) * 128] = hi
        g2[128:256, h * 128 : (h + 1) * 128] = (turned - hi.astype(F32)).astype(BF)
    local[1].wait()

    index = lax.broadcasted_iota(jnp.int32, (256, 128), 0).astype(F32)
    index = index.astype(BF)
    one, zero = jnp.ones((), BF), jnp.zeros((), BF)

    def gather(i, carry):
        cells = cv[pl.ds(pl.multiple_of(i * CH, CH), CH)]
        row = lax.shift_right_logical(cells, 7).astype(F32)
        lane = (cells & 127).astype(F32)
        table = g2[...]
        for b in range(CH // 2):
            hots = []
            for j in (2 * b, 2 * b + 1):
                at = slice(j * 128, (j + 1) * 128)
                hot = jnp.where(index == rows16(row[j : j + 1], 16), one, zero)
                oh[i, :, at] = hot
                oh8[i, :, at] = hot.astype(F8)
                mk[i, :, at] = jnp.where(index[:128] == rows16(lane[j : j + 1], 8), one, zero)
                hots.append(hot)
            found = jnp.dot(table, jnp.concatenate(hots, axis=1), preferred_element_type=F32)
            picked = (found[:128] + found[128:]) * mk[i, :, b * 256 : (b + 1) * 256].astype(F32)
            total = jnp.sum(jnp.sum(picked.reshape(16, 8, 256), axis=0), axis=0, keepdims=True)
            for j in range(2):
                gas[pl.ds(i * CH + 2 * b + j, 1), :] = total[:, j * 128 : (j + 1) * 128]
        return carry

    early = jnp.where(s == 0, EARLY, 0)
    lax.fori_loop(0, early, gather, 0)
    pl.semaphore_wait(barrier, 4)
    halo = [
        remote(state.at[pl.ds(155 * (1 - a), 5)], sx.at[pl.ds(165 * a, 5)], hsend.at[0], hrecv.at[0], (s, 1 - a, r)),
        remote(rsend, rrecv, hsend.at[1], hrecv.at[1], (s, a, 1 - r)),
        remote(upsend, uprecv, hsend.at[2], hrecv.at[2], (nxt, a, r)),
        remote(dnsend, dnrecv, hsend.at[3], hrecv.at[3], (prv, a, r)),
    ]
    for copy in (halo[0], halo[2], halo[3]):
        copy.start()

    def send_parcels(c, carry):
        parcel_copy(c).start()
        return carry

    lax.fori_loop(0, steps, send_parcels, 0)
    halo[1].start()


    lax.fori_loop(early, steps, gather, 0)

    @pl.when(a == 0)
    def _():
        sx[0:5] = jnp.zeros((5, 8, 128), F32)

    @pl.when(a == 1)
    def _():
        sx[165:170] = jnp.zeros((5, 8, 128), F32)

    for copy in (halo[0], halo[2], halo[3]):
        copy.wait_recv()
    sub = lax.broadcasted_iota(jnp.int32, (128, 128), 0)
    for q in range(10):
        both = jnp.where(
            sub == 0,
            (DIFFUSE + SWIRL) * uprecv[q : q + 1],
            jnp.where(sub == 127, DIFFUSE * dnrecv[q : q + 1], 0.0),
        )
        edge[16 * q : 16 * q + 16] = both.T.reshape(16, 8, 128)
    sub8 = lax.broadcasted_iota(jnp.int32, (8, 128), 0)
    lane8 = lax.broadcasted_iota(jnp.int32, (8, 128), 1)
    seam = sub8 == 7 * (1 - r)

    def flux(k):
        for u in range(5):
            i = k * 5 + u
            x = sx[5 + i]
            radial = jnp.where(sub8 == 0, 0.0, pltpu.roll(x, 1, 0)) + jnp.where(
                sub8 == 7, 0.0, pltpu.roll(x, 7, 0)
            )
            below = jnp.where(lane8 == 0, 0.0, pltpu.roll(x, 1, 1))
            above = jnp.where(lane8 == 127, 0.0, pltpu.roll(x, 127, 1))
            beside = (sx[i] + sx[i + 10]) + (radial + above)
            res[i] = (
                DIFFUSE * beside + (DIFFUSE + SWIRL) * below + edge[i] - (6.0 * DIFFUSE + SWIRL) * x
            )


    acc[...] = jnp.zeros_like(acc)
    live_count = count[0]

    def scatter(i, carry):
        parcel_copy(i).wait_recv()
        rows = pl.ds(pl.multiple_of(i * CH, CH), CH)
        fields = [pbuf[f, rows] for f in range(6)]
        slot = (lax.broadcasted_iota(jnp.int32, (CH, 128), 0) + i * CH) * 128 + lax.broadcasted_iota(
            jnp.int32, (CH, 128), 1
        )
        mass = jnp.where(slot < live_count, fields[0], 0.0)
        frac = 1.0 - jnp.exp(-fields[1] * (1.0 + 0.5 * jnp.tanh(gas[rows])))
        evap = mass * frac
        left[rows] = mass * (1.0 - frac)
        deposits = [evap] + [evap * fields[f] for f in range(2, 6)]
        for v in range(5):
            hi = deposits[v].astype(BF).astype(F32)
            low = (deposits[v] - hi) * LOW
            for j in range(CH):
                at = slice(j * 128, (j + 1) * 128)
                hot = mk[i, :, at]
                w[v * 128 : (v + 1) * 128, at] = hot * rows16(hi[j : j + 1], 8)
                w8[v * 128 : (v + 1) * 128, at] = (hot * rows16(low[j : j + 1], 8)).astype(F8)
        for k in range(32 // steps):
            flux(i * (32 // steps) + k)
        acc[:640] += lax.dot_general(w[...], oh[i], NT, preferred_element_type=F32)
        acc[640:] += lax.dot_general(w8[...], oh8[i], NT, preferred_element_type=F32)
        return carry

    lax.fori_loop(0, steps, scatter, 0)
    halo[1].wait_recv()
    for v in range(5):
        turned = (acc[v * 128 : (v + 1) * 128] + acc[640 + v * 128 : 768 + v * 128] * (1.0 / LOW)).T
        for k in range(32):
            i = k * 5 + v
            ring = jnp.where(seam, jnp.broadcast_to(DIFFUSE * rrecv[i : i + 1], (8, 128)), 0.0)
            res[i] += turned[8 * k : 8 * k + 8] + ring

    for copy in local[2:]:
        copy.wait()
    zeros = tuple(jnp.zeros((8, 128), F32) for _ in range(5))

    def product(jac, values):
        return [sum5([jac[u, v] * values[v] for v in range(5)]) for u in range(5)]

    def plane(k, carry, rate, jac, first, final):
        pushed = product(jac, carry)
        base = k * 5
        rk = rate[k]
        net = []
        for u in range(5):
            term = rk * pushed[u]
            r_u = res[base + u]
            if first:
                d = r_u - term
                tgt[base + u] = d
            else:
                d = tgt[base + u] - term
                if not final:
                    tgt[base + u] = r_u - term
            net.append(d)
        value = tuple(sum5([bv[k * 25 + u * 5 + v] * net[v] for v in range(5)]) for u in range(5))
        if final:
            for u in range(5):
                out[base + u] = sx[5 + base + u] + value[u]
        return value

    def relay(h):
        return remote(fsend.at[h], face.at[h], rlsend.at[h], rlrecv.at[h], (s, 1 - a, r))

    def half_sweep(hop, forward, first, final):
        sender = 0 if forward else 1

        @pl.when(a == 1 - sender)
        def _():
            relay(hop).wait_recv()

        @pl.when(a == sender)
        def _():
            face[hop] = jnp.zeros((5, 8, 128), F32)

        inflow = tuple(face[hop, u] for u in range(5))
        rate, jac = (lv, ljac) if forward else (uv, ujac)

        def body(i, carry):
            k = i if forward else 31 - i
            return plane(k, carry, rate, jac, first, final)

        last = lax.fori_loop(0, 32, body, inflow, unroll=4)

        @pl.when(a == sender)
        def _():
            for u in range(5):
                fsend[hop, u] = last[u]
            relay(hop).start()

    half_sweep(0, True, True, False)
    half_sweep(1, False, False, False)
    half_sweep(2, True, False, False)
    half_sweep(3, False, False, True)

    for hop in range(4):
        @pl.when(a == hop % 2)
        def _():
            relay(hop).wait_send()

    for copy in halo:
        copy.wait_send()

    def sent(c, carry):
        parcel_copy(c).wait_send()
        return carry

    lax.fori_loop(0, steps, sent, 0)


def solution(mesh):
    nsec = mesh.shape["sector"]

    def local(state, block_inverse, lower_rate, upper_rate, lower_jac, upper_jac, parcel_state, parcel_cell, parcel_count):
        hbm = pl.BlockSpec(memory_space=pl.ANY)
        vmem = pl.BlockSpec(memory_space=pltpu.VMEM)
        smem = pl.BlockSpec(memory_space=pltpu.SMEM)
        width = CH * 128
        dma = pltpu.SemaphoreType.DMA
        steps = 256 // CH
        out, left = pl.pallas_call(
            functools.partial(kernel, nsec),
            out_shape=(
                pltpu.VMEM((160, 8, 128), F32),
                pltpu.VMEM((256, 128), F32),
            ),
            in_specs=[hbm, hbm, hbm, hbm, smem, smem, hbm, hbm, smem],
            out_specs=(vmem, vmem),
            scratch_shapes=[
                pltpu.VMEM((170, 8, 128), F32),
                pltpu.VMEM((800, 8, 128), F32),
                pltpu.VMEM((32, 8, 128), F32),
                pltpu.VMEM((32, 8, 128), F32),
                pltpu.VMEM((256, 128), jnp.int32),
                pltpu.VMEM((6, 256, 128), F32),
                pltpu.VMEM((256, 128), F32),
                pltpu.VMEM((256, 256), BF),
                pltpu.VMEM((steps, 256, width), BF),
                pltpu.VMEM((steps, 256, width), F8),
                pltpu.VMEM((steps, 128, width), BF),
                pltpu.VMEM((640, width), BF),
                pltpu.VMEM((640, width), F8),
                pltpu.VMEM((1280, 256), F32),
                pltpu.VMEM((160, 8, 128), F32),
                pltpu.VMEM((160, 8, 128), F32),
                pltpu.VMEM((160, 8, 128), F32),
                pltpu.VMEM((160, 128), F32),
                pltpu.VMEM((160, 128), F32),
                pltpu.VMEM((16, 128), F32),
                pltpu.VMEM((16, 128), F32),
                pltpu.VMEM((16, 128), F32),
                pltpu.VMEM((16, 128), F32),
                pltpu.VMEM((4, 5, 8, 128), F32),
                pltpu.VMEM((4, 5, 8, 128), F32),
                dma((5,)),
                dma((steps,)),
                dma((steps,)),
                dma((4,)),
                dma((4,)),
                dma((4,)),
                dma((4,)),
            ],
            compiler_params=pltpu.CompilerParams(
                collective_id=0, has_side_effects=True, vmem_limit_bytes=56 << 20
            ),
        )(
            state.reshape(160, 8, 128),
            block_inverse.reshape(800, 8, 128),
            lower_rate,
            upper_rate,
            lower_jac,
            upper_jac,
            parcel_state.reshape(6, 256, 128),
            parcel_cell.reshape(256, 128),
            parcel_count.reshape(1),
        )
        return out.reshape(state.shape), left.reshape(parcel_cell.shape)

    return jax.shard_map(
        local,
        mesh=mesh,
        in_specs=(
            P("axial", None, "radial", "sector"),
            P("axial", None, None, "radial", "sector"),
            P("axial", "radial", "sector"),
            P("axial", "radial", "sector"),
            P(),
            P(),
            P(None, "axial", "radial", "sector"),
            P("axial", "radial", "sector"),
            P("axial", "radial", "sector"),
        ),
        out_specs=(P("axial", None, "radial", "sector"), P("axial", "radial", "sector")),
        check_vma=False,
    )
```

```python
import functools

import jax
import jax.numpy as jnp
from jax import lax
from jax.experimental import pallas as pl
from jax.experimental.pallas import tpu as pltpu
from jax.sharding import PartitionSpec as P

F32 = jnp.float32
BF = jnp.bfloat16
F8 = jnp.float8_e4m3fn
MESH = pl.DeviceIdType.MESH
NT = (((1,), (1,)), ((), ()))
DIFFUSE = 0.15
SWIRL = 0.6
CH = 32
EARLY = 4
LOW = 8192.0


def sum5(terms):
    return ((terms[0] + terms[1]) + (terms[2] + terms[3])) + terms[4]


def rows16(row, times):
    packed = jnp.broadcast_to(row, (16, 128)).astype(BF)
    return jnp.concatenate([packed] * times, axis=0)


def kernel(
    nsec,
    state, binv, lrate, urate, ljac, ujac, parcels, cell, count,
    out, left,
    sx, bv, lv, uv, cv, pbuf, gas, g2, oh, oh8, mk, w, w8, acc, res, tgt, phi, xs, edge,
    rsend, rrecv, upsend, uprecv, dnsend, dnrecv, face, fsend,
    lsem, psend, precv, hsend, hrecv, rlsend, rlrecv,
):
    s, a, r = lax.axis_index("sector"), lax.axis_index("axial"), lax.axis_index("radial")
    nxt, prv = lax.rem(s + 1, nsec), lax.rem(s + nsec - 1, nsec)
    steps = 256 // CH

    local = [
        pltpu.make_async_copy(state, sx.at[pl.ds(5, 160)], lsem.at[0]),
        pltpu.make_async_copy(cell, cv, lsem.at[1]),
        pltpu.make_async_copy(binv, bv, lsem.at[2]),
        pltpu.make_async_copy(lrate, lv, lsem.at[3]),
        pltpu.make_async_copy(urate, uv, lsem.at[4]),
    ]
    for copy in local:
        copy.start()

    barrier = pltpu.get_barrier_semaphore()
    for device in ((nxt, a, r), (prv, a, r), (s, 1 - a, r), (s, a, 1 - r)):
        pl.semaphore_signal(barrier, inc=1, device_id=device, device_id_type=MESH)

    def remote(src, dst, ssem, rsem, device):
        return pltpu.make_async_remote_copy(
            src_ref=src, dst_ref=dst, send_sem=ssem, recv_sem=rsem, device_id=device, device_id_type=MESH
        )

    def parcel_copy(c):
        rows = pl.ds(pl.multiple_of(c * CH, CH), CH)
        return remote(parcels.at[:, rows], pbuf.at[:, rows], psend.at[c], precv.at[c], (nxt, a, r))

    local[0].wait()

    for i in range(160):
        rsend[i : i + 1] = jnp.where(r == 0, sx[5 + i, 7:8, :], sx[5 + i, 0:1, :])
    for q in range(10):
        turned = sx[5 + 16 * q : 21 + 16 * q].reshape(128, 128).T
        upsend[q : q + 1] = turned[127:128]
        dnsend[q : q + 1] = turned[0:1]
    for h in range(2):
        tile = jnp.concatenate([sx[5 + (16 * h + k) * 5 + 4] for k in range(16)], axis=0)
        turned = tile.T
        hi = turned.astype(BF)
        g2[0:128, h * 128 : (h + 1) * 128] = hi
        g2[128:256, h * 128 : (h + 1) * 128] = (turned - hi.astype(F32)).astype(BF)
    local[1].wait()

    index = lax.broadcasted_iota(jnp.int32, (256, 128), 0).astype(F32)
    index = index.astype(BF)
    one, zero = jnp.ones((), BF), jnp.zeros((), BF)

    def gather(i, carry):
        cells = cv[pl.ds(pl.multiple_of(i * CH, CH), CH)]
        row = lax.shift_right_logical(cells, 7).astype(F32)
        lane = (cells & 127).astype(F32)
        table = g2[...]
        for b in range(CH // 2):
            hots = []
            for j in (2 * b, 2 * b + 1):
                at = slice(j * 128, (j + 1) * 128)
                hot = jnp.where(index == rows16(row[j : j + 1], 16), one, zero)
                oh[i, :, at] = hot
                oh8[i, :, at] = hot.astype(F8)
                mk[i, :, at] = jnp.where(index[:128] == rows16(lane[j : j + 1], 8), one, zero)
                hots.append(hot)
            found = jnp.dot(table, jnp.concatenate(hots, axis=1), preferred_element_type=F32)
            picked = (found[:128] + found[128:]) * mk[i, :, b * 256 : (b + 1) * 256].astype(F32)
            total = jnp.sum(jnp.sum(picked.reshape(16, 8, 256), axis=0), axis=0, keepdims=True)
            for j in range(2):
                gas[pl.ds(i * CH + 2 * b + j, 1), :] = total[:, j * 128 : (j + 1) * 128]
        return carry

    mix = [[jnp.where(a == 1, ljac[u, v], ujac[u, v]) for v in range(5)] for u in range(5)]
    for u in range(5):
        for v in range(5):
            phi[u * 5 + v] = jnp.full((8, 128), 1.0 if u == v else 0.0, F32)

    def influence(i):
        k = jnp.where(a == 1, i, 31 - i)
        rate = jnp.where(a == 1, lv[k], uv[k])
        for c in range(5):
            column = [phi[v * 5 + c] for v in range(5)]
            push = [rate * sum5([mix[u][v] * column[v] for v in range(5)]) for u in range(5)]
            for u in range(5):
                xs[k * 25 + u * 5 + c] = push[u]
                phi[u * 5 + c] = -sum5([bv[k * 25 + u * 5 + v] * push[v] for v in range(5)])

    def influence_planes(i, carry):
        for k in range(4):
            influence(i * 4 + k)
        return carry

    waits = lax.rem(s, 8) == 0

    @pl.when(waits)
    def _():
        for copy in local[2:]:
            copy.wait()
        lax.fori_loop(0, 8, influence_planes, 0)

    early = jnp.where(s == 0, EARLY, 0)
    lax.fori_loop(0, early, gather, 0)
    pl.semaphore_wait(barrier, 4)
    halo = [
        remote(state.at[pl.ds(155 * (1 - a), 5)], sx.at[pl.ds(165 * a, 5)], hsend.at[0], hrecv.at[0], (s, 1 - a, r)),
        remote(rsend, rrecv, hsend.at[1], hrecv.at[1], (s, a, 1 - r)),
        remote(upsend, uprecv, hsend.at[2], hrecv.at[2], (nxt, a, r)),
        remote(dnsend, dnrecv, hsend.at[3], hrecv.at[3], (prv, a, r)),
    ]
    for copy in (halo[0], halo[2], halo[3]):
        copy.start()

    def send_parcels(c, carry):
        parcel_copy(c).start()
        return carry

    lax.fori_loop(0, steps, send_parcels, 0)
    halo[1].start()


    @pl.when(jnp.logical_not(waits))
    def _():
        for copy in local[2:]:
            copy.wait()
        lax.fori_loop(0, 8, influence_planes, 0)

    lax.fori_loop(early, steps, gather, 0)

    @pl.when(a == 0)
    def _():
        sx[0:5] = jnp.zeros((5, 8, 128), F32)

    @pl.when(a == 1)
    def _():
        sx[165:170] = jnp.zeros((5, 8, 128), F32)

    for copy in (halo[0], halo[2], halo[3]):
        copy.wait_recv()
    sub = lax.broadcasted_iota(jnp.int32, (128, 128), 0)
    for q in range(10):
        both = jnp.where(
            sub == 0,
            (DIFFUSE + SWIRL) * uprecv[q : q + 1],
            jnp.where(sub == 127, DIFFUSE * dnrecv[q : q + 1], 0.0),
        )
        edge[16 * q : 16 * q + 16] = both.T.reshape(16, 8, 128)
    sub8 = lax.broadcasted_iota(jnp.int32, (8, 128), 0)
    lane8 = lax.broadcasted_iota(jnp.int32, (8, 128), 1)
    seam = sub8 == 7 * (1 - r)

    def flux(k):
        for u in range(5):
            i = k * 5 + u
            x = sx[5 + i]
            radial = jnp.where(sub8 == 0, 0.0, pltpu.roll(x, 1, 0)) + jnp.where(
                sub8 == 7, 0.0, pltpu.roll(x, 7, 0)
            )
            below = jnp.where(lane8 == 0, 0.0, pltpu.roll(x, 1, 1))
            above = jnp.where(lane8 == 127, 0.0, pltpu.roll(x, 127, 1))
            beside = (sx[i] + sx[i + 10]) + (radial + above)
            res[i] = (
                DIFFUSE * beside + (DIFFUSE + SWIRL) * below + edge[i] - (6.0 * DIFFUSE + SWIRL) * x
            )


    acc[...] = jnp.zeros_like(acc)
    live_count = count[0]

    def scatter(i, carry):
        parcel_copy(i).wait_recv()
        rows = pl.ds(pl.multiple_of(i * CH, CH), CH)
        fields = [pbuf[f, rows] for f in range(6)]
        slot = (lax.broadcasted_iota(jnp.int32, (CH, 128), 0) + i * CH) * 128 + lax.broadcasted_iota(
            jnp.int32, (CH, 128), 1
        )
        mass = jnp.where(slot < live_count, fields[0], 0.0)
        frac = 1.0 - jnp.exp(-fields[1] * (1.0 + 0.5 * jnp.tanh(gas[rows])))
        evap = mass * frac
        left[rows] = mass * (1.0 - frac)
        deposits = [evap] + [evap * fields[f] for f in range(2, 6)]
        his = [deposit.astype(BF).astype(F32) for deposit in deposits]
        lows = [(deposit - hi) * LOW for deposit, hi in zip(deposits, his)]
        for j in range(CH):
            at = slice(j * 128, (j + 1) * 128)
            hot = mk[i, :, at]
            for v in range(5):
                w[v * 128 : (v + 1) * 128, at] = hot * rows16(his[v][j : j + 1], 8)
                w8[v * 128 : (v + 1) * 128, at] = (hot * rows16(lows[v][j : j + 1], 8)).astype(F8)
        for k in range(32 // steps):
            flux(i * (32 // steps) + k)
        acc[:640] += lax.dot_general(w[...], oh[i], NT, preferred_element_type=F32)
        acc[640:] += lax.dot_general(w8[...], oh8[i], NT, preferred_element_type=F32)
        return carry

    lax.fori_loop(0, steps, scatter, 0)
    halo[1].wait_recv()
    for v in range(5):
        turned = (acc[v * 128 : (v + 1) * 128] + acc[640 + v * 128 : 768 + v * 128] * (1.0 / LOW)).T
        for k in range(32):
            i = k * 5 + v
            ring = jnp.where(seam, jnp.broadcast_to(DIFFUSE * rrecv[i : i + 1], (8, 128)), 0.0)
            res[i] += turned[8 * k : 8 * k + 8] + ring

    zeros = tuple(jnp.zeros((8, 128), F32) for _ in range(5))

    def product(jac, values):
        return [sum5([jac[u, v] * values[v] for v in range(5)]) for u in range(5)]

    def plane(k, carry, face, rate, jac, first, final):
        pushed = product(jac, carry)
        base = k * 5
        rk = rate[k]
        net = []
        for u in range(5):
            term = rk * pushed[u]
            r_u = res[base + u]
            if first:
                d = r_u - term
                tgt[base + u] = d
            else:
                d = (tgt[base + u] - sum5([xs[(base + u) * 5 + c] * face[c] for c in range(5)])) - term
                if not final:
                    tgt[base + u] = r_u - term
            net.append(d)
        value = tuple(sum5([bv[k * 25 + u * 5 + v] * net[v] for v in range(5)]) for u in range(5))
        if final:
            for u in range(5):
                out[base + u] = sx[5 + base + u] + value[u]
        return value

    def relay(h):
        return remote(fsend.at[h], face.at[h], rlsend.at[h], rlrecv.at[h], (s, 1 - a, r))

    def half_sweep(hop, forward, first, final):
        sender = 0 if forward else 1
        if not first:
            @pl.when(a == sender)
            def _():
                relay(hop - 1).wait_recv()

            @pl.when(a == 1 - sender)
            def _():
                face[hop - 1] = jnp.zeros((5, 8, 128), F32)
        if final:
            @pl.when(a == 1 - sender)
            def _():
                relay(hop).wait_recv()

            @pl.when(a == sender)
            def _():
                face[hop] = jnp.zeros((5, 8, 128), F32)

            inflow = tuple(face[hop, u] for u in range(5))
        else:
            inflow = zeros
        past = None if first else tuple(face[hop - 1, u] for u in range(5))
        rate, jac = (lv, ljac) if forward else (uv, ujac)

        def body(i, carry):
            k = i if forward else 31 - i
            return plane(k, carry, past, rate, jac, first, final)

        last = lax.fori_loop(0, 32, body, inflow, unroll=4)

        @pl.when(a == sender)
        def _():
            for u in range(5):
                fsend[hop, u] = last[u]
            relay(hop).start()

    half_sweep(0, True, True, False)
    half_sweep(1, False, False, False)
    half_sweep(2, True, False, False)
    half_sweep(3, False, False, True)

    for hop in range(4):
        @pl.when(a == hop % 2)
        def _():
            relay(hop).wait_send()

    for copy in halo:
        copy.wait_send()

    def sent(c, carry):
        parcel_copy(c).wait_send()
        return carry

    lax.fori_loop(0, steps, sent, 0)


def solution(mesh):
    nsec = mesh.shape["sector"]

    def local(state, block_inverse, lower_rate, upper_rate, lower_jac, upper_jac, parcel_state, parcel_cell, parcel_count):
        hbm = pl.BlockSpec(memory_space=pl.ANY)
        vmem = pl.BlockSpec(memory_space=pltpu.VMEM)
        smem = pl.BlockSpec(memory_space=pltpu.SMEM)
        width = CH * 128
        dma = pltpu.SemaphoreType.DMA
        steps = 256 // CH
        out, left = pl.pallas_call(
            functools.partial(kernel, nsec),
            out_shape=(
                pltpu.VMEM((160, 8, 128), F32),
                pltpu.VMEM((256, 128), F32),
            ),
            in_specs=[hbm, hbm, hbm, hbm, smem, smem, hbm, hbm, smem],
            out_specs=(vmem, vmem),
            scratch_shapes=[
                pltpu.VMEM((170, 8, 128), F32),
                pltpu.VMEM((800, 8, 128), F32),
                pltpu.VMEM((32, 8, 128), F32),
                pltpu.VMEM((32, 8, 128), F32),
                pltpu.VMEM((256, 128), jnp.int32),
                pltpu.VMEM((6, 256, 128), F32),
                pltpu.VMEM((256, 128), F32),
                pltpu.VMEM((256, 256), BF),
                pltpu.VMEM((steps, 256, width), BF),
                pltpu.VMEM((steps, 256, width), F8),
                pltpu.VMEM((steps, 128, width), BF),
                pltpu.VMEM((640, width), BF),
                pltpu.VMEM((640, width), F8),
                pltpu.VMEM((1280, 256), F32),
                pltpu.VMEM((160, 8, 128), F32),
                pltpu.VMEM((160, 8, 128), F32),
                pltpu.VMEM((25, 8, 128), F32),
                pltpu.VMEM((800, 8, 128), F32),
                pltpu.VMEM((160, 8, 128), F32),
                pltpu.VMEM((160, 128), F32),
                pltpu.VMEM((160, 128), F32),
                pltpu.VMEM((16, 128), F32),
                pltpu.VMEM((16, 128), F32),
                pltpu.VMEM((16, 128), F32),
                pltpu.VMEM((16, 128), F32),
                pltpu.VMEM((4, 5, 8, 128), F32),
                pltpu.VMEM((4, 5, 8, 128), F32),
                dma((5,)),
                dma((steps,)),
                dma((steps,)),
                dma((4,)),
                dma((4,)),
                dma((4,)),
                dma((4,)),
            ],
            compiler_params=pltpu.CompilerParams(
                collective_id=0, has_side_effects=True, vmem_limit_bytes=56 << 20
            ),
        )(
            state.reshape(160, 8, 128),
            block_inverse.reshape(800, 8, 128),
            lower_rate,
            upper_rate,
            lower_jac,
            upper_jac,
            parcel_state.reshape(6, 256, 128),
            parcel_cell.reshape(256, 128),
            parcel_count.reshape(1),
        )
        return out.reshape(state.shape), left.reshape(parcel_cell.shape)

    return jax.shard_map(
        local,
        mesh=mesh,
        in_specs=(
            P("axial", None, "radial", "sector"),
            P("axial", None, None, "radial", "sector"),
            P("axial", "radial", "sector"),
            P("axial", "radial", "sector"),
            P(),
            P(),
            P(None, "axial", "radial", "sector"),
            P("axial", "radial", "sector"),
            P("axial", "radial", "sector"),
        ),
        out_specs=(P("axial", None, "radial", "sector"), P("axial", "radial", "sector")),
        check_vma=False,
    )
```

```python
import functools

import jax
import jax.numpy as jnp
from jax import lax
from jax.experimental import pallas as pl
from jax.experimental.pallas import tpu as pltpu
from jax.sharding import PartitionSpec as P

F32 = jnp.float32
BF = jnp.bfloat16
F8 = jnp.float8_e4m3fn
MESH = pl.DeviceIdType.MESH
NT = (((1,), (1,)), ((), ()))
DIFFUSE = 0.15
SWIRL = 0.6
CH = 32
NEAR = 4
EARLY = 4
LOW = 8192.0


def sum5(terms):
    return ((terms[0] + terms[1]) + (terms[2] + terms[3])) + terms[4]


def rows16(row, times):
    packed = jnp.broadcast_to(row, (16, 128)).astype(BF)
    return jnp.concatenate([packed] * times, axis=0)


def kernel(
    nsec,
    state, binv, lrate, urate, ljac, ujac, parcels, cell, count,
    out, left,
    sx, bv, lv, uv, cv, pbuf, gas, g2, oh, oh8, mk, w, w8, acc, res, tgt, phi, xs, edge,
    rsend, rrecv, upsend, uprecv, dnsend, dnrecv, face, fsend,
    lsem, psend, precv, hsend, hrecv, rlsend, rlrecv,
):
    s, a, r = lax.axis_index("sector"), lax.axis_index("axial"), lax.axis_index("radial")
    nxt, prv = lax.rem(s + 1, nsec), lax.rem(s + nsec - 1, nsec)
    steps = 256 // CH

    local = [
        pltpu.make_async_copy(state, sx.at[pl.ds(5, 160)], lsem.at[0]),
        pltpu.make_async_copy(cell, cv, lsem.at[1]),
        pltpu.make_async_copy(binv, bv, lsem.at[2]),
        pltpu.make_async_copy(lrate, lv, lsem.at[3]),
        pltpu.make_async_copy(urate, uv, lsem.at[4]),
    ]
    for copy in local:
        copy.start()

    barrier = pltpu.get_barrier_semaphore()
    for device in ((nxt, a, r), (prv, a, r), (s, 1 - a, r), (s, a, 1 - r)):
        pl.semaphore_signal(barrier, inc=1, device_id=device, device_id_type=MESH)

    def remote(src, dst, ssem, rsem, device):
        return pltpu.make_async_remote_copy(
            src_ref=src, dst_ref=dst, send_sem=ssem, recv_sem=rsem, device_id=device, device_id_type=MESH
        )

    def parcel_copy(c):
        rows = pl.ds(pl.multiple_of(c * CH, CH), CH)
        return remote(parcels.at[:, rows], pbuf.at[:, rows], psend.at[c], precv.at[c], (nxt, a, r))

    local[0].wait()

    for i in range(160):
        rsend[i : i + 1] = jnp.where(r == 0, sx[5 + i, 7:8, :], sx[5 + i, 0:1, :])
    for q in range(10):
        turned = sx[5 + 16 * q : 21 + 16 * q].reshape(128, 128).T
        upsend[q : q + 1] = turned[127:128]
        dnsend[q : q + 1] = turned[0:1]
    for h in range(2):
        tile = jnp.concatenate([sx[5 + (16 * h + k) * 5 + 4] for k in range(16)], axis=0)
        turned = tile.T
        hi = turned.astype(BF)
        g2[0:128, h * 128 : (h + 1) * 128] = hi
        g2[128:256, h * 128 : (h + 1) * 128] = (turned - hi.astype(F32)).astype(BF)
    local[1].wait()

    index = lax.broadcasted_iota(jnp.int32, (256, 128), 0).astype(F32)
    index = index.astype(BF)
    one, zero = jnp.ones((), BF), jnp.zeros((), BF)

    def gather(i, carry):
        cells = cv[pl.ds(pl.multiple_of(i * CH, CH), CH)]
        row = lax.shift_right_logical(cells, 7).astype(F32)
        lane = (cells & 127).astype(F32)
        table = g2[...]
        for b in range(CH // 2):
            hots = []
            for j in (2 * b, 2 * b + 1):
                at = slice(j * 128, (j + 1) * 128)
                hot = jnp.where(index == rows16(row[j : j + 1], 16), one, zero)
                oh[i, :, at] = hot
                oh8[i, :, at] = hot.astype(F8)
                mk[i, :, at] = jnp.where(index[:128] == rows16(lane[j : j + 1], 8), one, zero)
                hots.append(hot)
            found = jnp.dot(table, jnp.concatenate(hots, axis=1), preferred_element_type=F32)
            picked = (found[:128] + found[128:]) * mk[i, :, b * 256 : (b + 1) * 256].astype(F32)
            total = jnp.sum(jnp.sum(picked.reshape(16, 8, 256), axis=0), axis=0, keepdims=True)
            for j in range(2):
                gas[pl.ds(i * CH + 2 * b + j, 1), :] = total[:, j * 128 : (j + 1) * 128]
        return carry

    mix = [[jnp.where(a == 1, ljac[u, v], ujac[u, v]) for v in range(5)] for u in range(5)]
    for u in range(5):
        for v in range(5):
            phi[u * 5 + v] = jnp.full((8, 128), 1.0 if u == v else 0.0, F32)

    def influence(i):
        k = jnp.where(a == 1, i, 31 - i)
        rate = jnp.where(a == 1, lv[k], uv[k])
        for c in range(5):
            column = [phi[v * 5 + c] for v in range(5)]
            push = [rate * sum5([mix[u][v] * column[v] for v in range(5)]) for u in range(5)]
            for u in range(5):
                xs[k * 25 + u * 5 + c] = push[u]
                phi[u * 5 + c] = -sum5([bv[k * 25 + u * 5 + v] * push[v] for v in range(5)])

    def influence_planes(i, carry):
        for k in range(4):
            influence(i * 4 + k)
        return carry

    waits = lax.rem(s, 8) == 0

    for copy in local[2:]:
        copy.wait()
    ahead = jnp.where(waits, 8, jnp.where(lax.rem(s, 8) == 7, 0, NEAR))
    lax.fori_loop(0, ahead, influence_planes, 0)

    early = jnp.where(s == 0, EARLY, 0)
    lax.fori_loop(0, early, gather, 0)
    pl.semaphore_wait(barrier, 4)
    halo = [
        remote(state.at[pl.ds(155 * (1 - a), 5)], sx.at[pl.ds(165 * a, 5)], hsend.at[0], hrecv.at[0], (s, 1 - a, r)),
        remote(rsend, rrecv, hsend.at[1], hrecv.at[1], (s, a, 1 - r)),
        remote(upsend, uprecv, hsend.at[2], hrecv.at[2], (nxt, a, r)),
        remote(dnsend, dnrecv, hsend.at[3], hrecv.at[3], (prv, a, r)),
    ]
    for copy in (halo[0], halo[2], halo[3]):
        copy.start()

    def send_parcels(c, carry):
        parcel_copy(c).start()
        return carry

    lax.fori_loop(0, steps, send_parcels, 0)
    halo[1].start()


    lax.fori_loop(ahead, 8, influence_planes, 0)
    lax.fori_loop(early, steps, gather, 0)

    @pl.when(a == 0)
    def _():
        sx[0:5] = jnp.zeros((5, 8, 128), F32)

    @pl.when(a == 1)
    def _():
        sx[165:170] = jnp.zeros((5, 8, 128), F32)

    for copy in (halo[0], halo[2], halo[3]):
        copy.wait_recv()
    sub = lax.broadcasted_iota(jnp.int32, (128, 128), 0)
    for q in range(10):
        both = jnp.where(
            sub == 0,
            (DIFFUSE + SWIRL) * uprecv[q : q + 1],
            jnp.where(sub == 127, DIFFUSE * dnrecv[q : q + 1], 0.0),
        )
        edge[16 * q : 16 * q + 16] = both.T.reshape(16, 8, 128)
    sub8 = lax.broadcasted_iota(jnp.int32, (8, 128), 0)
    lane8 = lax.broadcasted_iota(jnp.int32, (8, 128), 1)
    seam = sub8 == 7 * (1 - r)

    def flux(k):
        for u in range(5):
            i = k * 5 + u
            x = sx[5 + i]
            radial = jnp.where(sub8 == 0, 0.0, pltpu.roll(x, 1, 0)) + jnp.where(
                sub8 == 7, 0.0, pltpu.roll(x, 7, 0)
            )
            below = jnp.where(lane8 == 0, 0.0, pltpu.roll(x, 1, 1))
            above = jnp.where(lane8 == 127, 0.0, pltpu.roll(x, 127, 1))
            beside = (sx[i] + sx[i + 10]) + (radial + above)
            res[i] = (
                DIFFUSE * beside + (DIFFUSE + SWIRL) * below + edge[i] - (6.0 * DIFFUSE + SWIRL) * x
            )


    acc[...] = jnp.zeros_like(acc)
    live_count = count[0]

    def scatter(i, carry):
        parcel_copy(i).wait_recv()
        rows = pl.ds(pl.multiple_of(i * CH, CH), CH)
        fields = [pbuf[f, rows] for f in range(6)]
        slot = (lax.broadcasted_iota(jnp.int32, (CH, 128), 0) + i * CH) * 128 + lax.broadcasted_iota(
            jnp.int32, (CH, 128), 1
        )
        mass = jnp.where(slot < live_count, fields[0], 0.0)
        frac = 1.0 - jnp.exp(-fields[1] * (1.0 + 0.5 * jnp.tanh(gas[rows])))
        evap = mass * frac
        left[rows] = mass * (1.0 - frac)
        deposits = [evap] + [evap * fields[f] for f in range(2, 6)]
        his = [deposit.astype(BF).astype(F32) for deposit in deposits]
        lows = [(deposit - hi) * LOW for deposit, hi in zip(deposits, his)]
        for j in range(CH):
            at = slice(j * 128, (j + 1) * 128)
            hot = mk[i, :, at]
            for v in range(5):
                w[v * 128 : (v + 1) * 128, at] = hot * rows16(his[v][j : j + 1], 8)
                w8[v * 128 : (v + 1) * 128, at] = (hot * rows16(lows[v][j : j + 1], 8)).astype(F8)
        for k in range(32 // steps):
            flux(i * (32 // steps) + k)
        acc[:640] += lax.dot_general(w[...], oh[i], NT, preferred_element_type=F32)
        acc[640:] += lax.dot_general(w8[...], oh8[i], NT, preferred_element_type=F32)
        return carry

    lax.fori_loop(0, steps, scatter, 0)
    halo[1].wait_recv()
    for v in range(5):
        turned = (acc[v * 128 : (v + 1) * 128] + acc[640 + v * 128 : 768 + v * 128] * (1.0 / LOW)).T
        for k in range(32):
            i = k * 5 + v
            ring = jnp.where(seam, jnp.broadcast_to(DIFFUSE * rrecv[i : i + 1], (8, 128)), 0.0)
            res[i] += turned[8 * k : 8 * k + 8] + ring

    zeros = tuple(jnp.zeros((8, 128), F32) for _ in range(5))

    def product(jac, values):
        return [sum5([jac[u, v] * values[v] for v in range(5)]) for u in range(5)]

    def plane(k, carry, face, rate, jac, first, final):
        pushed = product(jac, carry)
        base = k * 5
        rk = rate[k]
        net = []
        for u in range(5):
            term = rk * pushed[u]
            r_u = res[base + u]
            if first:
                d = r_u - term
                tgt[base + u] = d
            else:
                d = (tgt[base + u] - sum5([xs[(base + u) * 5 + c] * face[c] for c in range(5)])) - term
                if not final:
                    tgt[base + u] = r_u - term
            net.append(d)
        value = tuple(sum5([bv[k * 25 + u * 5 + v] * net[v] for v in range(5)]) for u in range(5))
        if final:
            for u in range(5):
                out[base + u] = sx[5 + base + u] + value[u]
        return value

    def relay(h):
        return remote(fsend.at[h], face.at[h], rlsend.at[h], rlrecv.at[h], (s, 1 - a, r))

    def half_sweep(hop, forward, first, final):
        sender = 0 if forward else 1
        if not first:
            @pl.when(a == sender)
            def _():
                relay(hop - 1).wait_recv()

            @pl.when(a == 1 - sender)
            def _():
                face[hop - 1] = jnp.zeros((5, 8, 128), F32)
        if final:
            @pl.when(a == 1 - sender)
            def _():
                relay(hop).wait_recv()

            @pl.when(a == sender)
            def _():
                face[hop] = jnp.zeros((5, 8, 128), F32)

            inflow = tuple(face[hop, u] for u in range(5))
        else:
            inflow = zeros
        past = None if first else tuple(face[hop - 1, u] for u in range(5))
        rate, jac = (lv, ljac) if forward else (uv, ujac)

        def body(i, carry):
            k = i if forward else 31 - i
            return plane(k, carry, past, rate, jac, first, final)

        last = lax.fori_loop(0, 32, body, inflow, unroll=4)

        @pl.when(a == sender)
        def _():
            for u in range(5):
                fsend[hop, u] = last[u]
            relay(hop).start()

    half_sweep(0, True, True, False)
    half_sweep(1, False, False, False)
    half_sweep(2, True, False, False)
    half_sweep(3, False, False, True)

    for hop in range(4):
        @pl.when(a == hop % 2)
        def _():
            relay(hop).wait_send()

    for copy in halo:
        copy.wait_send()

    def sent(c, carry):
        parcel_copy(c).wait_send()
        return carry

    lax.fori_loop(0, steps, sent, 0)


def solution(mesh):
    nsec = mesh.shape["sector"]

    def local(state, block_inverse, lower_rate, upper_rate, lower_jac, upper_jac, parcel_state, parcel_cell, parcel_count):
        hbm = pl.BlockSpec(memory_space=pl.ANY)
        vmem = pl.BlockSpec(memory_space=pltpu.VMEM)
        smem = pl.BlockSpec(memory_space=pltpu.SMEM)
        width = CH * 128
        dma = pltpu.SemaphoreType.DMA
        steps = 256 // CH
        out, left = pl.pallas_call(
            functools.partial(kernel, nsec),
            out_shape=(
                pltpu.VMEM((160, 8, 128), F32),
                pltpu.VMEM((256, 128), F32),
            ),
            in_specs=[hbm, hbm, hbm, hbm, smem, smem, hbm, hbm, smem],
            out_specs=(vmem, vmem),
            scratch_shapes=[
                pltpu.VMEM((170, 8, 128), F32),
                pltpu.VMEM((800, 8, 128), F32),
                pltpu.VMEM((32, 8, 128), F32),
                pltpu.VMEM((32, 8, 128), F32),
                pltpu.VMEM((256, 128), jnp.int32),
                pltpu.VMEM((6, 256, 128), F32),
                pltpu.VMEM((256, 128), F32),
                pltpu.VMEM((256, 256), BF),
                pltpu.VMEM((steps, 256, width), BF),
                pltpu.VMEM((steps, 256, width), F8),
                pltpu.VMEM((steps, 128, width), BF),
                pltpu.VMEM((640, width), BF),
                pltpu.VMEM((640, width), F8),
                pltpu.VMEM((1280, 256), F32),
                pltpu.VMEM((160, 8, 128), F32),
                pltpu.VMEM((160, 8, 128), F32),
                pltpu.VMEM((25, 8, 128), F32),
                pltpu.VMEM((800, 8, 128), F32),
                pltpu.VMEM((160, 8, 128), F32),
                pltpu.VMEM((160, 128), F32),
                pltpu.VMEM((160, 128), F32),
                pltpu.VMEM((16, 128), F32),
                pltpu.VMEM((16, 128), F32),
                pltpu.VMEM((16, 128), F32),
                pltpu.VMEM((16, 128), F32),
                pltpu.VMEM((4, 5, 8, 128), F32),
                pltpu.VMEM((4, 5, 8, 128), F32),
                dma((5,)),
                dma((steps,)),
                dma((steps,)),
                dma((4,)),
                dma((4,)),
                dma((4,)),
                dma((4,)),
            ],
            compiler_params=pltpu.CompilerParams(
                collective_id=0, has_side_effects=True, vmem_limit_bytes=56 << 20
            ),
        )(
            state.reshape(160, 8, 128),
            block_inverse.reshape(800, 8, 128),
            lower_rate,
            upper_rate,
            lower_jac,
            upper_jac,
            parcel_state.reshape(6, 256, 128),
            parcel_cell.reshape(256, 128),
            parcel_count.reshape(1),
        )
        return out.reshape(state.shape), left.reshape(parcel_cell.shape)

    return jax.shard_map(
        local,
        mesh=mesh,
        in_specs=(
            P("axial", None, "radial", "sector"),
            P("axial", None, None, "radial", "sector"),
            P("axial", "radial", "sector"),
            P("axial", "radial", "sector"),
            P(),
            P(),
            P(None, "axial", "radial", "sector"),
            P("axial", "radial", "sector"),
            P("axial", "radial", "sector"),
        ),
        out_specs=(P("axial", None, "radial", "sector"), P("axial", "radial", "sector")),
        check_vma=False,
    )
```
